128 devices in a mesh: elem: 32 (over x, z, core), band: 4 (over y).
Axes of the slice: x: 4, y: 4, z: 4, core: 2. Of those that a mesh axis runs over, the one named last changes fastest.
Arguments:
- crm_state: bfloat16 [32, 128, 6, 3840], P('elem', 'band'), may hold values from -6 to 6
- host_state: float32 [72, 32, 128], P(None, 'elem', 'band'), may hold values from -6 to 6
- kappa: float32 [32, 128], P('elem', 'band'), may hold values from 0.02 to 0.2
- substeps: int32 [32, 128], P('elem', 'band'), may hold values from 1 to 4, as said below
- coupling: float32 [6, 6], replicated, may hold values from -2.5 to 2.5
- level_map: float32 [60, 72], replicated, may hold values from -0.75 to 0.75
- field_scale: float32 [6], replicated, may hold values from 0.5 to 1.5
- back_map: float32 [72, 60], replicated, may hold values from -0.75 to 0.75
- back_weight: float32 [6], replicated, may hold values from -3 to 3
Outputs:
- crm_final: bfloat16 [32, 128, 6, 3840], P('elem', 'band')
- host_final: float32 [72, 32, 128], P(None, 'elem', 'band')
The draws below stay inside these ranges and needn't reach their ends.
Inputs may be any that keep to these rules, and one draw needn't show every extreme that they name: Each aligned block of 1 x 32 columns (the columns of one device) draws a level from 1 to 4; each column of the block takes 1 plus a uniform integer modulo that level substeps. Column (0, 0) takes 4 substeps and column (0, 1) takes 1.
All inputs are finite; a program needn't handle non-finite values.
Results may differ from the reference program's by a relative error of at most 0.0055.
Values may be sent and summed in bfloat16 or wider, within the bound.
A program may use at most 128 MiB of HBM per device.

```python
import math
import jax
import jax.numpy as jnp
from jax import lax

LEV = 72
FIELDS = 6
NZC = 60
NXC = 64
SUB = 4
WINDOWS = 2
CXH = 1
CYH = 32
NGX = 32
NGY = 128


def draw_substeps(key, part):
    first_key, second_key = jax.random.split(jax.random.fold_in(key, 17))
    level = jax.random.randint(first_key, (NGX // CXH, NGY // CYH), 1, SUB + 1)
    level = jnp.repeat(jnp.repeat(level, CXH, axis=0), CYH, axis=1)
    raw = jax.random.randint(second_key, (NGX, NGY), 0, 1048576)
    counts = 1 + raw % level
    counts = counts.at[0, 0].set(SUB)
    counts = counts.at[0, 1].set(1)
    return counts.astype(jnp.int32)


def block_scale(rng, shape, shards, least, high):
    def one(axis_at, shards_of):
        draws = jax.random.uniform(jax.random.fold_in(jax.random.fold_in(rng, 6), axis_at), (shards_of,), jnp.float32, least / len(shards), high / len(shards))
        return jnp.repeat(jnp.exp(draws), shape[axis_at] // shards_of).reshape((-1,) + (1,) * (len(shape) - axis_at - 1))

    loudness = one(*shards[0])
    for cut in shards[1:]:
        loudness = loudness * one(*cut)
    return loudness


def normal_values(stream_key, dims, width, most, pieces=(), held_as=jnp.bfloat16):
    values = width * jax.random.normal(stream_key, dims, jnp.float32)
    if pieces:
        values = values * block_scale(stream_key, dims, pieces, -0.22, 0.18)
    return jnp.clip(values, -most, most).astype(held_as)


def setup_inputs(seed: int = 0) -> dict:
    keys = jax.random.split(jax.random.key(seed), 10)
    crm_state = normal_values(keys[0], (NGX, NGY, FIELDS, NZC * NXC), 1.0, 6.0, ((0, 32), (1, 4)))
    host_state = normal_values(keys[1], (LEV, NGX, NGY), 1.0, 6.0, ((1, 32), (2, 4)), jnp.float32)
    kappa = jnp.clip(jnp.exp(math.log(0.2) - 2.3025851 * jax.random.uniform(keys[2], (NGX, NGY), jnp.float32) ** block_scale(keys[2], (NGX, NGY), ((0, 32), (1, 4)), -0.2, 0.2)), 0.02, 0.2)
    substeps = draw_substeps(jax.random.fold_in(keys[9], 71), 0)
    coupling = normal_values(keys[4], (FIELDS, FIELDS), FIELDS ** -0.5, 2.5, (), jnp.float32)
    level_map = normal_values(keys[5], (NZC, LEV), LEV ** -0.5, 0.75, (), jnp.float32)
    field_scale = jnp.clip(jax.random.uniform(keys[6], (FIELDS,), jnp.float32, 0.5, 1.5), 0.5, 1.5)
    back_map = normal_values(keys[7], (LEV, NZC), NZC ** -0.5, 0.75, (), jnp.float32)
    back_weight = normal_values(keys[8], (FIELDS,), 1.0, 3.0, (), jnp.float32)
    return dict(crm_state=crm_state, host_state=host_state, kappa=kappa, substeps=substeps, coupling=coupling, level_map=level_map, field_scale=field_scale, back_map=back_map, back_weight=back_weight)


cloud_step = 0.1
return_scale = 1.0


def cloud_substep(fields, forcing, coupling, active):
    highest = lax.Precision.HIGHEST
    wind = fields[:, 0]
    deriv = 0.5 * (jnp.roll(fields, -1, axis=3) - jnp.roll(fields, 1, axis=3))
    padded = jnp.pad(fields, ((0, 0), (0, 0), (1, 1), (0, 0)))
    vertical = padded[:, :, 2:] - 2.0 * fields + padded[:, :, :-2]
    mixing = jnp.tanh(jnp.einsum('fg,ngzx->nfzx', coupling, fields, precision=highest))
    change = cloud_step * (-wind[:, None] * deriv + vertical + mixing + forcing[..., None])
    return fields + jnp.where(active[:, None, None, None], change, 0.0)


def host_section(host, tend, kappa):
    def face(host_near, kappa_near):
        return 0.5 * (kappa + kappa_near) * (host_near - host)
    spread = face(jnp.roll(host, -1, 1), jnp.roll(kappa, -1, 0)) + face(jnp.roll(host, 1, 1), jnp.roll(kappa, 1, 0))
    spread = spread + face(jnp.roll(host, -1, 2), jnp.roll(kappa, -1, 1)) + face(jnp.roll(host, 1, 2), jnp.roll(kappa, 1, 1))
    return host + (tend + spread)


def reference(crm_state, host_state, kappa, substeps, coupling, level_map, field_scale, back_map, back_weight):
    highest = lax.Precision.HIGHEST
    cloud = crm_state.astype(jnp.float32).reshape(NGX, NGY, FIELDS, NZC, NXC)
    host = host_state
    for window in range(WINDOWS):
        columns = jnp.transpose(host, (1, 2, 0))

        def run_row(items):
            fields, column_row, counts = items
            mapped = jnp.einsum('zl,nl->nz', level_map, column_row, precision=highest)
            forcing = field_scale[None, :, None] * mapped[:, None, :]
            start = fields
            for turn in range(SUB):
                fields = cloud_substep(fields, forcing, coupling, counts > turn)
            mean = jnp.mean(fields - start, axis=-1)
            mixed = jnp.einsum('f,nfz->nz', back_weight, mean, precision=highest)
            tend = return_scale * jnp.einsum('lz,nz->nl', back_map, mixed, precision=highest)
            return fields, tend

        cloud, tend = lax.map(run_row, (cloud, columns, substeps))
        host = host_section(host, jnp.transpose(tend, (2, 0, 1)), kappa)
    crm_final = cloud.reshape(NGX, NGY, FIELDS, NZC * NXC).astype(jnp.bfloat16)
    return crm_final, host
```

```python
import jax
import jax.numpy as jnp
from jax import lax
from jax.experimental import pallas as pl
from jax.experimental.pallas import tpu as pltpu
from jax.sharding import PartitionSpec as P

LEV = 72
FIELDS = 6
NZC = 60
NXC = 64
SUB = 4
WINDOWS = 2
COLS = 32
ROWS = FIELDS * COLS
BLOCKS = 15
LANES = 256
TILES = 30
CELLS = NZC * NXC
STEP = 0.1
MESH = pl.DeviceIdType.MESH
F32 = jnp.float32
BF16 = jnp.bfloat16
HIGHEST = lax.Precision.HIGHEST
NT = (((1,), (1,)), ((), ()))


def iota(shape, axis):
    return lax.broadcasted_iota(jnp.int32, shape, axis)


def to_column(row):
    eye = iota((COLS, COLS), 0) == iota((COLS, COLS), 1)
    return jnp.sum(jnp.where(eye, jnp.broadcast_to(row, (COLS, COLS)), 0.0), axis=1, keepdims=True)


def swap_halves(tile):
    return pltpu.roll(tile, 64, 1)


def kernel(
    crm_in, host_in, kappa_in, counts_in, level_in, back_in, coup, scale, weight,
    crm_out, host_out,
    xbuf, obuf, sa, sb, force, qsum, kron, deriv, level2, back2, host, halo_e, halo_b,
    in_sem, out_sem, send_sem, recv_sem,
):
    elem, band = lax.axis_index("elem"), lax.axis_index("band")
    n_elem, n_band = lax.axis_size("elem"), lax.axis_size("band")
    up_e = (lax.rem(elem + 1, n_elem), band)
    dn_e = (lax.rem(elem + n_elem - 1, n_elem), band)
    up_b = (elem, lax.rem(band + 1, n_band))
    dn_b = (elem, lax.rem(band + n_band - 1, n_band))

    barrier = pltpu.get_barrier_semaphore()
    for other in (up_e, dn_e, up_b, dn_b):
        pl.semaphore_signal(barrier, inc=1, device_id=other, device_id_type=MESH)

    loads = [pltpu.make_async_copy(crm_in.at[f], xbuf.at[f], in_sem.at[f]) for f in range(FIELDS)]
    for copy in loads:
        copy.start()

    kcol = to_column(kappa_in[...])
    ccol = to_column(counts_in[...].astype(F32))
    lane = iota((COLS, 128), 1)
    host[0] = jnp.where(lane == LEV, jnp.broadcast_to(kcol, (COLS, 128)), 0.0)
    host[0, :, 0:LEV] = host_in[...]

    pl.semaphore_wait(barrier, 4)

    def exchange(window):
        src = host.at[window]
        copies = []
        for i, (other, part, dst) in enumerate((
            (up_e, src, halo_e.at[window, 0]),
            (dn_e, src, halo_e.at[window, 1]),
            (up_b, src.at[pl.ds(COLS - 8, 8)], halo_b.at[window, 0]),
            (dn_b, src.at[pl.ds(0, 8)], halo_b.at[window, 1]),
        )):
            copies.append(pltpu.make_async_remote_copy(
                src_ref=part, dst_ref=dst,
                send_sem=send_sem.at[window, i], recv_sem=recv_sem.at[window, i],
                device_id=other, device_id_type=MESH,
            ))
        return copies

    copies = exchange(0)
    for copy in copies:
        copy.start()

    level2[...] = jnp.zeros_like(level2)
    level2[0:NZC, :] = level_in[...]
    level2[64 : 64 + NZC, :] = level_in[...]
    back2[...] = jnp.zeros_like(back2)
    back2[0:LEV, 0:NZC] = back_in[...]
    row_c = iota((COLS, ROWS), 0)
    lane_r = iota((COLS, ROWS), 1)
    for f in range(FIELDS):
        value = jnp.zeros((COLS, ROWS), F32)
        for g in range(FIELDS):
            value = jnp.where(lane_r == row_c + g * COLS, coup[f, g], value)
        kron[f * COLS : (f + 1) * COLS, :] = value.astype(BF16)
    src = iota((LANES, LANES), 0)
    dst = iota((LANES, LANES), 1)
    same = (src // NXC) == (dst // NXC)
    ahead = jnp.logical_and(same, (src % NXC) == (dst + 1) % NXC)
    behind = jnp.logical_and(same, (dst % NXC) == (src + 1) % NXC)
    deriv[...] = (jnp.where(behind, 0.5, 0.0) - jnp.where(ahead, 0.5, 0.0)).astype(BF16)

    low = iota((COLS, 128), 1) < NXC
    for f in range(FIELDS):
        loads[f].wait()
        rows = slice(f * COLS, (f + 1) * COLS)
        for j in range(BLOCKS):
            for half in range(2):
                za, zb = 30 * half + j, 30 * half + 15 + j
                ta = xbuf[f, :, (za // 2) * 128 : (za // 2 + 1) * 128]
                tb = xbuf[f, :, (zb // 2) * 128 : (zb // 2 + 1) * 128]
                if j % 2 == 0:
                    tile = jnp.where(low, ta, tb)
                else:
                    tile = swap_halves(jnp.where(low, tb, ta))
                sa[j, rows, half * 128 : (half + 1) * 128] = tile.astype(F32)

    def weighted(j):
        total = weight[0] * sa[j, 0:COLS, :]
        for f in range(1, FIELDS):
            total = total + weight[f] * sa[j, f * COLS : (f + 1) * COLS, :]
        return total

    for j in range(BLOCKS):
        qsum[j] = weighted(j)

    lane_q = iota((COLS, LANES), 1)

    def shift_up(value):
        moved = pltpu.roll(value, NXC, 1)
        return jnp.where(lane_q < NXC, 0.0, moved)

    def shift_down(value):
        moved = pltpu.roll(value, LANES - NXC, 1)
        return jnp.where(lane_q >= LANES - NXC, 0.0, moved)

    cnt = jnp.broadcast_to(ccol, (COLS, LANES))

    def substep(src_ref, dst_ref, turn):
        a = jnp.where(cnt > turn.astype(F32), STEP, 0.0)
        keep = 1.0 - 2.0 * a
        for j in range(BLOCKS):
            state = src_ref[j]
            packed = state.astype(BF16)
            mix = jnp.dot(kron[...], packed, preferred_element_type=F32)
            slope = jnp.dot(packed, deriv[...], preferred_element_type=F32)
            wind = state[0:COLS]
            for f in range(FIELDS):
                rows = slice(f * COLS, (f + 1) * COLS)
                above = src_ref[j + 1, rows] if j < BLOCKS - 1 else shift_down(src_ref[0, rows])
                below = src_ref[j - 1, rows] if j > 0 else shift_up(src_ref[BLOCKS - 1, rows])
                total = (above + below) + (jnp.tanh(mix[rows]) + force[j, rows]) + wind * slope[rows]
                dst_ref[j, rows] = keep * state[rows] + a * total

    zq = iota((128, LANES), 0)
    lq = iota((128, LANES), 1)
    spread_lanes = jnp.where((zq % 64) == 15 * (lq // NXC), 1.0, 0.0).astype(BF16)
    rq = iota((LANES, 128), 0)
    cq = iota((LANES, 128), 1)
    gather_lanes = jnp.where(cq == 15 * (rq // NXC), 1.0 / NXC, 0.0).astype(BF16)
    sub_row = iota((COLS, 128), 0)

    for window in range(WINDOWS):
        hval = host[window]
        mapped = lax.dot_general(hval[:, 0:LEV], level2[...], NT, precision=HIGHEST, preferred_element_type=F32)
        high = mapped.astype(BF16).astype(F32)
        mhl = jnp.where(lane < 64, high, mapped - high)
        stack = jnp.concatenate([mhl] + [pltpu.roll(mhl, 128 - j, 1) for j in range(1, BLOCKS)], axis=0)
        cells = jnp.dot(stack.astype(BF16), spread_lanes, preferred_element_type=F32)
        for j in range(BLOCKS):
            for f in range(FIELDS):
                force[j, f * COLS : (f + 1) * COLS, :] = scale[f] * cells[j * COLS : (j + 1) * COLS, :]

        def turns(i, carry):
            substep(sa, sb, 2 * i)
            substep(sb, sa, 2 * i + 1)
            return carry

        lax.fori_loop(0, SUB // 2, turns, 0)

        parts = []
        for j in range(BLOCKS):
            now = weighted(j)
            parts.append((now - qsum[j]).astype(BF16))
            qsum[j] = now
        means = jnp.dot(jnp.concatenate(parts, axis=0), gather_lanes, preferred_element_type=F32)
        mixed = means[0:COLS]
        for j in range(1, BLOCKS):
            mixed = mixed + pltpu.roll(means[j * COLS : (j + 1) * COLS], j, 1)
        tend = lax.dot_general(mixed, back2[...], NT, precision=HIGHEST, preferred_element_type=F32)

        for copy in copies:
            copy.wait()
        kmid = jnp.broadcast_to(kcol, (COLS, 128))

        def face(near):
            knear = jnp.broadcast_to(near[:, LEV : LEV + 1], (COLS, 128))
            return 0.5 * (kmid + knear) * (near - hval)

        prev = pltpu.roll(hval, 1, 0)
        prev = jnp.where(sub_row == 0, jnp.broadcast_to(halo_b[window, 0, 7:8, :], (COLS, 128)), prev)
        nxt = pltpu.roll(hval, COLS - 1, 0)
        nxt = jnp.where(sub_row == COLS - 1, jnp.broadcast_to(halo_b[window, 1, 0:1, :], (COLS, 128)), nxt)
        flux = face(halo_e[window, 1]) + face(halo_e[window, 0])
        flux = flux + face(nxt) + face(prev)
        hnew = hval + (tend + flux)
        if window < WINDOWS - 1:
            host[window + 1] = jnp.where(lane == LEV, kmid, hnew)
            copies = exchange(window + 1)
            for copy in copies:
                copy.start()
        else:
            host_out[...] = hnew[:, 0:LEV]

    stores = [pltpu.make_async_copy(obuf.at[f], crm_out.at[f], out_sem.at[f]) for f in range(FIELDS)]
    for f in range(FIELDS):
        rows = slice(f * COLS, (f + 1) * COLS)
        tiles = {}
        for j in range(BLOCKS):
            for half in range(2):
                tile = sa[j, rows, half * 128 : (half + 1) * 128].astype(BF16)
                tiles[j, half] = tile if j % 2 == 0 else swap_halves(tile)
        for t in range(TILES):
            za, zb = 2 * t, 2 * t + 1
            ta = tiles[za % 15, za // 30]
            tb = tiles[zb % 15, zb // 30]
            obuf[f, :, t * 128 : (t + 1) * 128] = jnp.where(low, ta, tb)
        stores[f].start()
    for copy in stores:
        copy.wait()


def body(
    crm_state, host_state, kappa, substeps, coupling, level_map, field_scale, back_map, back_weight
):
    crm = jnp.transpose(crm_state[0], (1, 0, 2))
    host = jnp.transpose(host_state[:, 0, :], (1, 0))
    vmem = pl.BlockSpec(memory_space=pltpu.VMEM)
    smem = pl.BlockSpec(memory_space=pltpu.SMEM)
    anym = pl.BlockSpec(memory_space=pl.ANY)
    crm_final, host_final = pl.pallas_call(
        kernel,
        out_shape=(
            jax.ShapeDtypeStruct((FIELDS, COLS, CELLS), BF16),
            jax.ShapeDtypeStruct((COLS, LEV), F32),
        ),
        in_specs=[anym, vmem, vmem, vmem, vmem, vmem, smem, smem, smem],
        out_specs=(anym, vmem),
        scratch_shapes=[
            pltpu.VMEM((FIELDS, COLS, CELLS), BF16),
            pltpu.VMEM((FIELDS, COLS, CELLS), BF16),
            pltpu.VMEM((BLOCKS, ROWS, LANES), F32),
            pltpu.VMEM((BLOCKS, ROWS, LANES), F32),
            pltpu.VMEM((BLOCKS, ROWS, LANES), F32),
            pltpu.VMEM((BLOCKS, COLS, LANES), F32),
            pltpu.VMEM((ROWS, ROWS), BF16),
            pltpu.VMEM((LANES, LANES), BF16),
            pltpu.VMEM((128, LEV), F32),
            pltpu.VMEM((128, 128), F32),
            pltpu.VMEM((WINDOWS, COLS, 128), F32),
            pltpu.VMEM((WINDOWS, 2, COLS, 128), F32),
            pltpu.VMEM((WINDOWS, 2, 8, 128), F32),
            pltpu.SemaphoreType.DMA((FIELDS,)),
            pltpu.SemaphoreType.DMA((FIELDS,)),
            pltpu.SemaphoreType.DMA((WINDOWS, 4)),
            pltpu.SemaphoreType.DMA((WINDOWS, 4)),
        ],
        compiler_params=pltpu.CompilerParams(
            collective_id=0, has_side_effects=True, vmem_limit_bytes=48 * 1024 * 1024
        ),
    )(crm, host, kappa, substeps, level_map, back_map, coupling, field_scale, back_weight)
    return (
        jnp.transpose(crm_final, (1, 0, 2))[None],
        jnp.transpose(host_final, (1, 0))[:, None, :],
    )


def solution(mesh):
    return jax.shard_map(
        body,
        mesh=mesh,
        in_specs=(
            P("elem", "band", None, None),
            P(None, "elem", "band"),
            P("elem", "band"),
            P("elem", "band"),
            P(),
            P(),
            P(),
            P(),
            P(),
        ),
        out_specs=(P("elem", "band", None, None), P(None, "elem", "band")),
        check_vma=False,
    )
```

```python
import jax
import jax.numpy as jnp
from jax import lax
from jax.experimental import pallas as pl
from jax.experimental.pallas import tpu as pltpu
from jax.sharding import PartitionSpec as P

LEV = 72
FIELDS = 6
NZC = 60
NXC = 64
SUB = 4
WINDOWS = 2
COLS = 32
ROWS = FIELDS * COLS
BLOCKS = 15
LANES = 256
TILES = 30
CELLS = NZC * NXC
STEP = 0.1
MESH = pl.DeviceIdType.MESH
F32 = jnp.float32
BF16 = jnp.bfloat16
HIGHEST = lax.Precision.HIGHEST
NT = (((1,), (1,)), ((), ()))


def iota(shape, axis):
    return lax.broadcasted_iota(jnp.int32, shape, axis)


def to_column(row):
    eye = iota((COLS, COLS), 0) == iota((COLS, COLS), 1)
    return jnp.sum(jnp.where(eye, jnp.broadcast_to(row, (COLS, COLS)), 0.0), axis=1, keepdims=True)


def swap_halves(tile):
    return pltpu.roll(tile, 64, 1)


def kernel(
    crm_in, host_in, kappa_in, counts_in, level_in, back_in, coup_in, scale_in, weight_in,
    sa, dq, host_base, back2,
    xbuf, sb, force, qsum, kron, deriv, level2, host, halo_e, halo_b,
    hbuf, kbuf, cbuf, lbuf, bbuf, coup, scale, weight,
    in_sem, arg_sem, send_sem, recv_sem,
):
    elem, band = lax.axis_index("elem"), lax.axis_index("band")
    n_elem, n_band = lax.axis_size("elem"), lax.axis_size("band")
    up_e = (lax.rem(elem + 1, n_elem), band)
    dn_e = (lax.rem(elem + n_elem - 1, n_elem), band)
    up_b = (elem, lax.rem(band + 1, n_band))
    dn_b = (elem, lax.rem(band + n_band - 1, n_band))

    small = [
        pltpu.make_async_copy(src, dst, arg_sem.at[i])
        for i, (src, dst) in enumerate((
            (host_in, hbuf), (level_in, lbuf), (scale_in, scale), (kappa_in, kbuf), (counts_in, cbuf),
            (weight_in, weight), (coup_in, coup), (back_in, bbuf),
        ))
    ]
    for copy in small:
        copy.start()
    loads = [pltpu.make_async_copy(crm_in.at[f], xbuf.at[f], in_sem.at[f]) for f in range(FIELDS)]
    for copy in loads:
        copy.start()

    barrier = pltpu.get_barrier_semaphore()
    for other in (up_e, dn_e, up_b, dn_b):
        pl.semaphore_signal(barrier, inc=1, device_id=other, device_id_type=MESH)

    def exchange(window):
        src = host.at[window]
        copies = []
        for i, (other, part, dst) in enumerate((
            (up_e, src, halo_e.at[window, 0]),
            (dn_e, src, halo_e.at[window, 1]),
            (up_b, src.at[pl.ds(COLS - 8, 8)], halo_b.at[window, 0]),
            (dn_b, src.at[pl.ds(0, 8)], halo_b.at[window, 1]),
        )):
            copies.append(pltpu.make_async_remote_copy(
                src_ref=part, dst_ref=dst,
                send_sem=send_sem.at[window, i], recv_sem=recv_sem.at[window, i],
                device_id=other, device_id_type=MESH,
            ))
        return copies

    level2[...] = jnp.zeros_like(level2)
    back2[...] = jnp.zeros_like(back2)
    src = iota((LANES, LANES), 0)
    dst = iota((LANES, LANES), 1)
    same = (src // NXC) == (dst // NXC)
    ahead = jnp.logical_and(same, (src % NXC) == (dst + 1) % NXC)
    behind = jnp.logical_and(same, (dst % NXC) == (src + 1) % NXC)
    deriv[...] = (jnp.where(behind, 0.5, 0.0) - jnp.where(ahead, 0.5, 0.0)).astype(BF16)
    zq = iota((128, LANES), 0)
    lq = iota((128, LANES), 1)
    spread_lanes = jnp.where((zq % 64) == 15 * (lq // NXC), 1.0, 0.0).astype(BF16)
    sub_row = iota((COLS, 128), 0)
    lane = iota((COLS, 128), 1)
    lane_q = iota((COLS, LANES), 1)
    low = lane < NXC

    for copy in small:
        copy.wait()

    kcol = to_column(kbuf[...])
    ccol = to_column(cbuf[...].astype(F32))
    kmid = jnp.broadcast_to(kcol, (COLS, 128))
    host[0] = jnp.where(lane == LEV, kmid, 0.0)
    host[0, :, 0:LEV] = hbuf[...]
    level2[0:NZC, :] = lbuf[...]
    level2[64 : 64 + NZC, :] = lbuf[...]
    back2[0:NZC, 0:LEV] = bbuf[...]
    row_c = iota((COLS, ROWS), 0)
    lane_r = iota((COLS, ROWS), 1)
    for f in range(FIELDS):
        value = jnp.zeros((COLS, ROWS), F32)
        for g in range(FIELDS):
            value = jnp.where(lane_r == row_c + g * COLS, coup[f, g], value)
        kron[f * COLS : (f + 1) * COLS, :] = value.astype(BF16)

    def forcing(window):
        hval = host[window]
        mapped = lax.dot_general(hval[:, 0:LEV], level2[...], NT, precision=HIGHEST, preferred_element_type=F32)
        high = mapped.astype(BF16).astype(F32)
        mhl = jnp.where(low, high, mapped - high)
        stack = jnp.concatenate([mhl] + [pltpu.roll(mhl, 128 - j, 1) for j in range(1, BLOCKS)], axis=0)
        cells = jnp.dot(stack.astype(BF16), spread_lanes, preferred_element_type=F32)
        for j in range(BLOCKS):
            for f in range(FIELDS):
                force[j, f * COLS : (f + 1) * COLS, :] = scale[f] * cells[j * COLS : (j + 1) * COLS, :]

    forcing(0)

    for f in range(FIELDS):
        loads[f].wait()
        rows = slice(f * COLS, (f + 1) * COLS)
        for j in range(BLOCKS):
            for half in range(2):
                za, zb = 30 * half + j, 30 * half + 15 + j
                ta = xbuf[f, :, (za // 2) * 128 : (za // 2 + 1) * 128]
                tb = xbuf[f, :, (zb // 2) * 128 : (zb // 2 + 1) * 128]
                if j % 2 == 0:
                    tile = jnp.where(low, ta, tb)
                else:
                    tile = swap_halves(jnp.where(low, tb, ta))
                sa[j, rows, half * 128 : (half + 1) * 128] = tile.astype(F32)

    def weighted(j):
        total = weight[0] * sa[j, 0:COLS, :]
        for f in range(1, FIELDS):
            total = total + weight[f] * sa[j, f * COLS : (f + 1) * COLS, :]
        return total

    for j in range(BLOCKS):
        qsum[j] = weighted(j)

    def shift_up(value):
        moved = pltpu.roll(value, NXC, 1)
        return jnp.where(lane_q < NXC, 0.0, moved)

    def shift_down(value):
        moved = pltpu.roll(value, LANES - NXC, 1)
        return jnp.where(lane_q >= LANES - NXC, 0.0, moved)

    cnt = jnp.broadcast_to(ccol, (COLS, LANES))

    def substep(src_ref, dst_ref, turn):
        a = jnp.where(cnt > turn.astype(F32), STEP, 0.0)
        keep = 1.0 - 2.0 * a
        for j in range(BLOCKS):
            state = src_ref[j]
            packed = state.astype(BF16)
            mix = jnp.dot(kron[...], packed, preferred_element_type=F32)
            slope = jnp.dot(packed, deriv[...], preferred_element_type=F32)
            wind = state[0:COLS]
            for f in range(FIELDS):
                rows = slice(f * COLS, (f + 1) * COLS)
                above = src_ref[j + 1, rows] if j < BLOCKS - 1 else shift_down(src_ref[0, rows])
                below = src_ref[j - 1, rows] if j > 0 else shift_up(src_ref[BLOCKS - 1, rows])
                total = (above + below) + (jnp.tanh(mix[rows]) + force[j, rows]) + wind * slope[rows]
                dst_ref[j, rows] = keep * state[rows] + a * total

    def fluxes(window, hval):
        def face(near):
            knear = jnp.broadcast_to(near[:, LEV : LEV + 1], (COLS, 128))
            return 0.5 * (kmid + knear) * (near - hval)

        prev = pltpu.roll(hval, 1, 0)
        prev = jnp.where(sub_row == 0, jnp.broadcast_to(halo_b[window, 0, 7:8, :], (COLS, 128)), prev)
        nxt = pltpu.roll(hval, COLS - 1, 0)
        nxt = jnp.where(sub_row == COLS - 1, jnp.broadcast_to(halo_b[window, 1, 0:1, :], (COLS, 128)), nxt)
        flux = face(halo_e[window, 1]) + face(halo_e[window, 0])
        return flux + face(nxt) + face(prev)

    def turns0(i, carry):
        @pl.when(i == 1)
        def _():
            pl.semaphore_wait(barrier, 4)
            for copy in exchange(0):
                copy.start()

        substep(sa, sb, 2 * i)
        substep(sb, sa, 2 * i + 1)
        return carry

    lax.fori_loop(0, SUB // 2, turns0, 0)

    for j in range(BLOCKS):
        now = weighted(j)
        dq[j] = (now - qsum[j]).astype(BF16)
        qsum[j] = now
    for copy in exchange(0):
        copy.wait()
    hval = host[0]
    tend = tendency(dq, back2)
    hnew = hval + (tend + fluxes(0, hval))
    host[1] = jnp.where(lane == LEV, kmid, hnew)
    copies = exchange(1)
    for copy in copies:
        copy.start()
    forcing(1)

    def turns1(i, carry):
        substep(sa, sb, 2 * i)
        substep(sb, sa, 2 * i + 1)
        return carry

    lax.fori_loop(0, SUB // 2, turns1, 0)

    for j in range(BLOCKS):
        dq[j] = (weighted(j) - qsum[j]).astype(BF16)
    for copy in copies:
        copy.wait()
    hval = host[1]
    host_base[0] = hval
    host_base[1] = fluxes(1, hval)


def tendency(dq, back2):
    rq = iota((LANES, 128), 0)
    cq = iota((LANES, 128), 1)
    gather_lanes = jnp.where(cq == 15 * (rq // NXC), 1.0 / NXC, 0.0).astype(BF16)
    parts = jnp.concatenate([dq[j] for j in range(BLOCKS)], axis=0)
    means = jnp.dot(parts, gather_lanes, preferred_element_type=F32)
    mixed = means[0:COLS]
    for j in range(1, BLOCKS):
        mixed = mixed + pltpu.roll(means[j * COLS : (j + 1) * COLS], j, 1)
    return jnp.dot(mixed, back2[...], precision=HIGHEST, preferred_element_type=F32)


def finish(sfin, dq, host_base, back2, crm_out, host_out, obuf, hbuf, out_sem, host_sem):
    low = iota((COLS, 128), 1) < NXC
    stores = [pltpu.make_async_copy(obuf.at[f], crm_out.at[f], out_sem.at[f]) for f in range(FIELDS)]
    for f in range(FIELDS):
        rows = slice(f * COLS, (f + 1) * COLS)
        tiles = {}
        for j in range(BLOCKS):
            for half in range(2):
                tile = sfin[j, rows, half * 128 : (half + 1) * 128].astype(BF16)
                tiles[j, half] = tile if j % 2 == 0 else swap_halves(tile)
        for t in range(TILES):
            za, zb = 2 * t, 2 * t + 1
            ta = tiles[za % 15, za // 30]
            tb = tiles[zb % 15, zb // 30]
            obuf[f, :, t * 128 : (t + 1) * 128] = jnp.where(low, ta, tb)
        stores[f].start()
    tend = tendency(dq, back2)
    hbuf[...] = (host_base[0] + (tend + host_base[1]))[:, 0:LEV]
    last = pltpu.make_async_copy(hbuf, host_out, host_sem)
    last.start()
    for copy in stores:
        copy.wait()
    last.wait()


def body(
    crm_state, host_state, kappa, substeps, coupling, level_map, field_scale, back_map, back_weight
):
    crm = jnp.transpose(crm_state[0], (1, 0, 2))
    host = jnp.transpose(host_state[:, 0, :], (1, 0))
    back = jnp.transpose(back_map, (1, 0))
    vmem = pl.BlockSpec(memory_space=pltpu.VMEM)
    hbm = pl.BlockSpec(memory_space=pltpu.HBM)
    middle = pl.pallas_call(
        kernel,
        out_shape=(
            jax.ShapeDtypeStruct((BLOCKS, ROWS, LANES), F32),
            jax.ShapeDtypeStruct((BLOCKS, COLS, LANES), BF16),
            jax.ShapeDtypeStruct((2, COLS, 128), F32),
            jax.ShapeDtypeStruct((128, 128), F32),
        ),
        in_specs=[hbm] * 9,
        out_specs=(vmem,) * 4,
        scratch_shapes=[
            pltpu.VMEM((FIELDS, COLS, CELLS), BF16),
            pltpu.VMEM((BLOCKS, ROWS, LANES), F32),
            pltpu.VMEM((BLOCKS, ROWS, LANES), F32),
            pltpu.VMEM((BLOCKS, COLS, LANES), F32),
            pltpu.VMEM((ROWS, ROWS), BF16),
            pltpu.VMEM((LANES, LANES), BF16),
            pltpu.VMEM((128, LEV), F32),
            pltpu.VMEM((WINDOWS, COLS, 128), F32),
            pltpu.VMEM((WINDOWS, 2, COLS, 128), F32),
            pltpu.VMEM((WINDOWS, 2, 8, 128), F32),
            pltpu.VMEM((COLS, LEV), F32),
            pltpu.VMEM((1, COLS), F32),
            pltpu.VMEM((1, COLS), jnp.int32),
            pltpu.VMEM((NZC, LEV), F32),
            pltpu.VMEM((NZC, LEV), F32),
            pltpu.SMEM((FIELDS, FIELDS), F32),
            pltpu.SMEM((FIELDS,), F32),
            pltpu.SMEM((FIELDS,), F32),
            pltpu.SemaphoreType.DMA((FIELDS,)),
            pltpu.SemaphoreType.DMA((8,)),
            pltpu.SemaphoreType.DMA((WINDOWS, 4)),
            pltpu.SemaphoreType.DMA((WINDOWS, 4)),
        ],
        compiler_params=pltpu.CompilerParams(
            collective_id=0, has_side_effects=True, vmem_limit_bytes=40 * 1024 * 1024
        ),
    )(*(
        pltpu.with_memory_space_constraint(x, pltpu.HBM)
        for x in (crm, host, kappa, substeps, level_map, back, coupling, field_scale, back_weight)
    ))
    crm_final, host_final = pl.pallas_call(
        finish,
        out_shape=(
            jax.ShapeDtypeStruct((FIELDS, COLS, CELLS), BF16),
            jax.ShapeDtypeStruct((COLS, LEV), F32),
        ),
        in_specs=[vmem] * 4,
        out_specs=(hbm, hbm),
        scratch_shapes=[
            pltpu.VMEM((FIELDS, COLS, CELLS), BF16),
            pltpu.VMEM((COLS, LEV), F32),
            pltpu.SemaphoreType.DMA((FIELDS,)),
            pltpu.SemaphoreType.DMA,
        ],
        compiler_params=pltpu.CompilerParams(vmem_limit_bytes=16 * 1024 * 1024),
    )(*middle)
    return (
        jnp.transpose(crm_final, (1, 0, 2))[None],
        jnp.transpose(host_final, (1, 0))[:, None, :],
    )


def solution(mesh):
    return jax.shard_map(
        body,
        mesh=mesh,
        in_specs=(
            P("elem", "band", None, None),
            P(None, "elem", "band"),
            P("elem", "band"),
            P("elem", "band"),
            P(),
            P(),
            P(),
            P(),
            P(),
        ),
        out_specs=(P("elem", "band", None, None), P(None, "elem", "band")),
        check_vma=False,
    )
```

```python
import jax
import jax.numpy as jnp
from jax import lax
from jax.experimental import pallas as pl
from jax.experimental.pallas import tpu as pltpu
from jax.sharding import PartitionSpec as P

LEV = 72
FIELDS = 6
NZC = 60
NXC = 64
SUB = 4
WINDOWS = 2
COLS = 32
ROWS = FIELDS * COLS
BLOCKS = 15
LANES = 256
TILES = 30
CELLS = NZC * NXC
STEP = 0.1
MESH = pl.DeviceIdType.MESH
F32 = jnp.float32
BF16 = jnp.bfloat16
HIGHEST = lax.Precision.HIGHEST
NT = (((1,), (1,)), ((), ()))


def iota(shape, axis):
    return lax.broadcasted_iota(jnp.int32, shape, axis)


def to_column(row):
    eye = iota((COLS, COLS), 0) == iota((COLS, COLS), 1)
    return jnp.sum(jnp.where(eye, jnp.broadcast_to(row, (COLS, COLS)), 0.0), axis=1, keepdims=True)


def swap_halves(tile):
    return pltpu.roll(tile, 64, 1)


def kernel(
    crm_in, host_in, kappa_in, counts_in, level_in, back_in, coup_in, scale_in, weight_in,
    sa, dq, host_base, back2,
    xbuf, sb, force, qsum, kron, deriv, level2, host, halo_e, halo_b,
    hbuf, kbuf, cbuf, lbuf, bbuf, coup, scale, weight,
    in_sem, arg_sem, send_sem, recv_sem,
):
    elem, band = lax.axis_index("elem"), lax.axis_index("band")
    n_elem, n_band = lax.axis_size("elem"), lax.axis_size("band")
    up_e = (lax.rem(elem + 1, n_elem), band)
    dn_e = (lax.rem(elem + n_elem - 1, n_elem), band)
    up_b = (elem, lax.rem(band + 1, n_band))
    dn_b = (elem, lax.rem(band + n_band - 1, n_band))

    small = [
        pltpu.make_async_copy(src, dst, arg_sem.at[i])
        for i, (src, dst) in enumerate((
            (host_in, hbuf), (level_in, lbuf), (scale_in, scale), (kappa_in, kbuf), (counts_in, cbuf),
            (weight_in, weight), (coup_in, coup), (back_in, bbuf),
        ))
    ]
    for copy in small:
        copy.start()
    loads = [pltpu.make_async_copy(crm_in.at[f], xbuf.at[f], in_sem.at[f]) for f in range(FIELDS)]
    for copy in loads:
        copy.start()

    barrier = pltpu.get_barrier_semaphore()
    for other in (up_e, dn_e, up_b, dn_b):
        pl.semaphore_signal(barrier, inc=1, device_id=other, device_id_type=MESH)

    def exchange(window):
        src = host.at[window]
        copies = []
        for i, (other, part, dst) in enumerate((
            (up_e, src, halo_e.at[window, 0]),
            (dn_e, src, halo_e.at[window, 1]),
            (up_b, src.at[pl.ds(COLS - 8, 8)], halo_b.at[window, 0]),
            (dn_b, src.at[pl.ds(0, 8)], halo_b.at[window, 1]),
        )):
            copies.append(pltpu.make_async_remote_copy(
                src_ref=part, dst_ref=dst,
                send_sem=send_sem.at[window, i], recv_sem=recv_sem.at[window, i],
                device_id=other, device_id_type=MESH,
            ))
        return copies

    level2[...] = jnp.zeros_like(level2)
    back2[...] = jnp.zeros_like(back2)
    src = iota((LANES, LANES), 0)
    dst = iota((LANES, LANES), 1)
    same = (src // NXC) == (dst // NXC)
    ahead = jnp.logical_and(same, (src % NXC) == (dst + 1) % NXC)
    behind = jnp.logical_and(same, (dst % NXC) == (src + 1) % NXC)
    deriv[...] = (jnp.where(behind, 0.5, 0.0) - jnp.where(ahead, 0.5, 0.0)).astype(BF16)
    zq = iota((128, LANES), 0)
    lq = iota((128, LANES), 1)
    spread_lanes = jnp.where((zq % 64) == 15 * (lq // NXC), 1.0, 0.0).astype(BF16)
    sub_row = iota((COLS, 128), 0)
    lane = iota((COLS, 128), 1)
    lane_q = iota((COLS, LANES), 1)
    low = lane < NXC

    for copy in small:
        copy.wait()

    kcol = to_column(kbuf[...])
    ccol = to_column(cbuf[...].astype(F32))
    kmid = jnp.broadcast_to(kcol, (COLS, 128))
    host[0] = jnp.where(lane == LEV, kmid, 0.0)
    host[0, :, 0:LEV] = hbuf[...]
    level2[0:NZC, :] = lbuf[...]
    level2[64 : 64 + NZC, :] = lbuf[...]
    back2[0:NZC, 0:LEV] = bbuf[...]
    row_c = iota((COLS, ROWS), 0)
    lane_r = iota((COLS, ROWS), 1)
    for f in range(FIELDS):
        value = jnp.zeros((COLS, ROWS), F32)
        for g in range(FIELDS):
            value = jnp.where(lane_r == row_c + g * COLS, coup[f, g], value)
        kron[f * COLS : (f + 1) * COLS, :] = value.astype(BF16)

    def forcing(window):
        hval = host[window]
        mapped = lax.dot_general(hval[:, 0:LEV], level2[...], NT, precision=HIGHEST, preferred_element_type=F32)
        high = mapped.astype(BF16).astype(F32)
        mhl = jnp.where(low, high, mapped - high)
        stack = jnp.concatenate([mhl] + [pltpu.roll(mhl, 128 - j, 1) for j in range(1, BLOCKS)], axis=0)
        cells = jnp.dot(stack.astype(BF16), spread_lanes, preferred_element_type=F32)
        for j in range(BLOCKS):
            for f in range(FIELDS):
                force[j, f * COLS : (f + 1) * COLS, :] = scale[f] * cells[j * COLS : (j + 1) * COLS, :]

    forcing(0)

    for f in range(FIELDS):
        loads[f].wait()
        rows = slice(f * COLS, (f + 1) * COLS)
        for j in range(BLOCKS):
            for half in range(2):
                za, zb = 30 * half + j, 30 * half + 15 + j
                ta = xbuf[f, :, (za // 2) * 128 : (za // 2 + 1) * 128]
                tb = xbuf[f, :, (zb // 2) * 128 : (zb // 2 + 1) * 128]
                if j % 2 == 0:
                    tile = jnp.where(low, ta, tb)
                else:
                    tile = swap_halves(jnp.where(low, tb, ta))
                sa[j, rows, half * 128 : (half + 1) * 128] = tile.astype(F32)

    def weighted(j):
        total = weight[0] * sa[j, 0:COLS, :]
        for f in range(1, FIELDS):
            total = total + weight[f] * sa[j, f * COLS : (f + 1) * COLS, :]
        return total

    for j in range(BLOCKS):
        qsum[j] = weighted(j)

    def shift_up(value):
        moved = pltpu.roll(value, NXC, 1)
        return jnp.where(lane_q < NXC, 0.0, moved)

    def shift_down(value):
        moved = pltpu.roll(value, LANES - NXC, 1)
        return jnp.where(lane_q >= LANES - NXC, 0.0, moved)

    cnt = jnp.broadcast_to(ccol, (COLS, LANES))

    def substep(src_ref, dst_ref, turn):
        a = jnp.where(cnt > turn.astype(F32), STEP, 0.0)
        keep = 1.0 - 2.0 * a

        for j0 in range(0, BLOCKS, 5):
            packed = jnp.concatenate([src_ref[j].astype(BF16) for j in range(j0, j0 + 5)], axis=0)
            slopes = jnp.dot(packed, deriv[...], preferred_element_type=F32)
            for j in range(j0, j0 + 5):
                mix = jnp.dot(kron[...], packed[(j - j0) * ROWS : (j - j0 + 1) * ROWS], preferred_element_type=F32)
                slope = slopes[(j - j0) * ROWS : (j - j0 + 1) * ROWS]
                wind = src_ref[j, 0:COLS]
                for f in range(FIELDS):
                    rows = slice(f * COLS, (f + 1) * COLS)
                    above = src_ref[j + 1, rows] if j < BLOCKS - 1 else shift_down(src_ref[0, rows])
                    below = src_ref[j - 1, rows] if j > 0 else shift_up(src_ref[BLOCKS - 1, rows])
                    total = (above + below) + (jnp.tanh(mix[rows]) + force[j, rows]) + wind * slope[rows]
                    dst_ref[j, rows] = keep * src_ref[j, rows] + a * total

    def fluxes(window, hval):
        def face(near):
            knear = jnp.broadcast_to(near[:, LEV : LEV + 1], (COLS, 128))
            return 0.5 * (kmid + knear) * (near - hval)

        prev = pltpu.roll(hval, 1, 0)
        prev = jnp.where(sub_row == 0, jnp.broadcast_to(halo_b[window, 0, 7:8, :], (COLS, 128)), prev)
        nxt = pltpu.roll(hval, COLS - 1, 0)
        nxt = jnp.where(sub_row == COLS - 1, jnp.broadcast_to(halo_b[window, 1, 0:1, :], (COLS, 128)), nxt)
        flux = face(halo_e[window, 1]) + face(halo_e[window, 0])
        return flux + face(nxt) + face(prev)

    def turns0(i, carry):
        substep(sa, sb, 2 * i)
        substep(sb, sa, 2 * i + 1)
        return carry

    pl.semaphore_wait(barrier, 4)
    for copy in exchange(0):
        copy.start()
    lax.fori_loop(0, SUB // 2, turns0, 0)

    for j in range(BLOCKS):
        now = weighted(j)
        dq[j] = (now - qsum[j]).astype(BF16)
        qsum[j] = now
    for copy in exchange(0):
        copy.wait()
    hval = host[0]
    tend = tendency(dq, back2)
    hnew = hval + (tend + fluxes(0, hval))
    host[1] = jnp.where(lane == LEV, kmid, hnew)
    copies = exchange(1)
    for copy in copies:
        copy.start()
    forcing(1)

    def turns1(i, carry):
        substep(sa, sb, 2 * i)
        substep(sb, sa, 2 * i + 1)
        return carry

    lax.fori_loop(0, SUB // 2, turns1, 0)

    for j in range(BLOCKS):
        dq[j] = (weighted(j) - qsum[j]).astype(BF16)
    for copy in copies:
        copy.wait()
    hval = host[1]
    host_base[0] = hval
    host_base[1] = fluxes(1, hval)


def tendency(dq, back2):
    rq = iota((LANES, 128), 0)
    cq = iota((LANES, 128), 1)
    gather_lanes = jnp.where(cq == 15 * (rq // NXC), 1.0 / NXC, 0.0).astype(BF16)
    parts = jnp.concatenate([dq[j] for j in range(BLOCKS)], axis=0)
    means = jnp.dot(parts, gather_lanes, preferred_element_type=F32)
    mixed = means[0:COLS]
    for j in range(1, BLOCKS):
        mixed = mixed + pltpu.roll(means[j * COLS : (j + 1) * COLS], j, 1)
    return jnp.dot(mixed, back2[...], precision=HIGHEST, preferred_element_type=F32)


def finish(sfin, dq, host_base, back2, crm_out, host_out, obuf, hbuf, out_sem, host_sem):
    low = iota((COLS, 128), 1) < NXC
    stores = [pltpu.make_async_copy(obuf.at[f], crm_out.at[f], out_sem.at[f]) for f in range(FIELDS)]
    for f in range(FIELDS):
        rows = slice(f * COLS, (f + 1) * COLS)
        tiles = {}
        for j in range(BLOCKS):
            for half in range(2):
                tile = sfin[j, rows, half * 128 : (half + 1) * 128].astype(BF16)
                tiles[j, half] = tile if j % 2 == 0 else swap_halves(tile)
        for t in range(TILES):
            za, zb = 2 * t, 2 * t + 1
            ta = tiles[za % 15, za // 30]
            tb = tiles[zb % 15, zb // 30]
            obuf[f, :, t * 128 : (t + 1) * 128] = jnp.where(low, ta, tb)
        stores[f].start()
    tend = tendency(dq, back2)
    hbuf[...] = (host_base[0] + (tend + host_base[1]))[:, 0:LEV]
    last = pltpu.make_async_copy(hbuf, host_out, host_sem)
    last.start()
    for copy in stores:
        copy.wait()
    last.wait()


def body(
    crm_state, host_state, kappa, substeps, coupling, level_map, field_scale, back_map, back_weight
):
    crm = jnp.transpose(crm_state[0], (1, 0, 2))
    host = jnp.transpose(host_state[:, 0, :], (1, 0))
    back = jnp.transpose(back_map, (1, 0))
    vmem = pl.BlockSpec(memory_space=pltpu.VMEM)
    hbm = pl.BlockSpec(memory_space=pltpu.HBM)
    middle = pl.pallas_call(
        kernel,
        out_shape=(
            jax.ShapeDtypeStruct((BLOCKS, ROWS, LANES), F32),
            jax.ShapeDtypeStruct((BLOCKS, COLS, LANES), BF16),
            jax.ShapeDtypeStruct((2, COLS, 128), F32),
            jax.ShapeDtypeStruct((128, 128), F32),
        ),
        in_specs=[hbm] * 9,
        out_specs=(vmem,) * 4,
        scratch_shapes=[
            pltpu.VMEM((FIELDS, COLS, CELLS), BF16),
            pltpu.VMEM((BLOCKS, ROWS, LANES), F32),
            pltpu.VMEM((BLOCKS, ROWS, LANES), F32),
            pltpu.VMEM((BLOCKS, COLS, LANES), F32),
            pltpu.VMEM((ROWS, ROWS), BF16),
            pltpu.VMEM((LANES, LANES), BF16),
            pltpu.VMEM((128, LEV), F32),
            pltpu.VMEM((WINDOWS, COLS, 128), F32),
            pltpu.VMEM((WINDOWS, 2, COLS, 128), F32),
            pltpu.VMEM((WINDOWS, 2, 8, 128), F32),
            pltpu.VMEM((COLS, LEV), F32),
            pltpu.VMEM((1, COLS), F32),
            pltpu.VMEM((1, COLS), jnp.int32),
            pltpu.VMEM((NZC, LEV), F32),
            pltpu.VMEM((NZC, LEV), F32),
            pltpu.SMEM((FIELDS, FIELDS), F32),
            pltpu.SMEM((FIELDS,), F32),
            pltpu.SMEM((FIELDS,), F32),
            pltpu.SemaphoreType.DMA((FIELDS,)),
            pltpu.SemaphoreType.DMA((8,)),
            pltpu.SemaphoreType.DMA((WINDOWS, 4)),
            pltpu.SemaphoreType.DMA((WINDOWS, 4)),
        ],
        compiler_params=pltpu.CompilerParams(
            collective_id=0, has_side_effects=True, vmem_limit_bytes=40 * 1024 * 1024
        ),
    )(*(
        pltpu.with_memory_space_constraint(x, pltpu.HBM)
        for x in (crm, host, kappa, substeps, level_map, back, coupling, field_scale, back_weight)
    ))
    crm_final, host_final = pl.pallas_call(
        finish,
        out_shape=(
            jax.ShapeDtypeStruct((FIELDS, COLS, CELLS), BF16),
            jax.ShapeDtypeStruct((COLS, LEV), F32),
        ),
        in_specs=[vmem] * 4,
        out_specs=(hbm, hbm),
        scratch_shapes=[
            pltpu.VMEM((FIELDS, COLS, CELLS), BF16),
            pltpu.VMEM((COLS, LEV), F32),
            pltpu.SemaphoreType.DMA((FIELDS,)),
            pltpu.SemaphoreType.DMA,
        ],
        compiler_params=pltpu.CompilerParams(vmem_limit_bytes=16 * 1024 * 1024),
    )(*middle)
    return (
        jnp.transpose(crm_final, (1, 0, 2))[None],
        jnp.transpose(host_final, (1, 0))[:, None, :],
    )


def solution(mesh):
    return jax.shard_map(
        body,
        mesh=mesh,
        in_specs=(
            P("elem", "band", None, None),
            P(None, "elem", "band"),
            P("elem", "band"),
            P("elem", "band"),
            P(),
            P(),
            P(),
            P(),
            P(),
        ),
        out_specs=(P("elem", "band", None, None), P(None, "elem", "band")),
        check_vma=False,
    )
```

```python
import jax
import jax.numpy as jnp
from jax import lax
from jax.experimental import pallas as pl
from jax.experimental.pallas import tpu as pltpu
from jax.sharding import PartitionSpec as P

LEV = 72
FIELDS = 6
NZC = 60
NXC = 64
SUB = 4
WINDOWS = 2
COLS = 32
ROWS = FIELDS * COLS
BLOCKS = 15
LANES = 256
TILES = 30
CELLS = NZC * NXC
STEP = 0.1
MESH = pl.DeviceIdType.MESH
F32 = jnp.float32
BF16 = jnp.bfloat16
NT = (((1,), (1,)), ((), ()))


def iota(shape, axis):
    return lax.broadcasted_iota(jnp.int32, shape, axis)


def to_column(row):
    eye = iota((COLS, COLS), 0) == iota((COLS, COLS), 1)
    return jnp.sum(jnp.where(eye, jnp.broadcast_to(row, (COLS, COLS)), 0.0), axis=1, keepdims=True)


def swap_halves(tile):
    return pltpu.roll(tile, 64, 1)


def kernel(
    crm_in, host_in, kappa_in, counts_in, level_in, back_in, coup_in, scale_in, weight_in,
    obuf, host_fin,
    xbuf, sa, sb, dq, back2, force, qsum, kron, deriv, level2, square, host, halo_e, halo_b,
    hbuf, kbuf, cbuf, lbuf, bbuf, coup, scale, weight,
    in_sem, arg_sem, send_sem, recv_sem,
):
    elem, band = lax.axis_index("elem"), lax.axis_index("band")
    n_elem, n_band = lax.axis_size("elem"), lax.axis_size("band")
    up_e = (lax.rem(elem + 1, n_elem), band)
    dn_e = (lax.rem(elem + n_elem - 1, n_elem), band)
    up_b = (elem, lax.rem(band + 1, n_band))
    dn_b = (elem, lax.rem(band + n_band - 1, n_band))

    small = [
        pltpu.make_async_copy(src, dst, arg_sem.at[i])
        for i, (src, dst) in enumerate((
            (host_in, hbuf), (level_in, lbuf), (scale_in, scale), (kappa_in, kbuf), (counts_in, cbuf),
            (weight_in, weight), (coup_in, coup), (back_in, bbuf),
        ))
    ]
    for copy in small:
        copy.start()
    loads = [pltpu.make_async_copy(crm_in.at[f], xbuf.at[f], in_sem.at[f]) for f in range(FIELDS)]
    for copy in loads:
        copy.start()

    barrier = pltpu.get_barrier_semaphore()
    for other in (up_e, dn_e, up_b, dn_b):
        pl.semaphore_signal(barrier, inc=1, device_id=other, device_id_type=MESH)

    def exchange(window):
        src = host.at[window]
        copies = []
        for i, (other, part, dst) in enumerate((
            (up_e, src, halo_e.at[window, 0]),
            (dn_e, src, halo_e.at[window, 1]),
            (up_b, src.at[pl.ds(COLS - 8, 8)], halo_b.at[window, 0]),
            (dn_b, src.at[pl.ds(0, 8)], halo_b.at[window, 1]),
        )):
            copies.append(pltpu.make_async_remote_copy(
                src_ref=part, dst_ref=dst,
                send_sem=send_sem.at[window, i], recv_sem=recv_sem.at[window, i],
                device_id=other, device_id_type=MESH,
            ))
        return copies

    def send_borders():
        pl.semaphore_wait(barrier, 4)
        for copy in exchange(0):
            copy.start()

    pad_l = jnp.zeros((128, 128), F32)
    src = iota((LANES, LANES), 0)
    dst = iota((LANES, LANES), 1)
    same = (src // NXC) == (dst // NXC)
    ahead = jnp.logical_and(same, (src % NXC) == (dst + 1) % NXC)
    behind = jnp.logical_and(same, (dst % NXC) == (src + 1) % NXC)
    deriv[...] = (jnp.where(behind, 0.5, 0.0) - jnp.where(ahead, 0.5, 0.0)).astype(BF16)
    zq = iota((128, LANES), 0)
    lq = iota((128, LANES), 1)
    spread_lanes = jnp.where((zq % 64) == 15 * (lq // NXC), 1.0, 0.0).astype(BF16)
    sub_row = iota((COLS, 128), 0)
    lane = iota((COLS, 128), 1)
    lane_q = iota((COLS, LANES), 1)
    low = lane < NXC

    for copy in small:
        copy.wait()

    kcol = to_column(kbuf[...])
    ccol = to_column(cbuf[...].astype(F32))
    kmid = jnp.broadcast_to(kcol, (COLS, 128))
    host[0] = jnp.where(lane == LEV, kmid, 0.0)
    host[0, :, 0:LEV] = hbuf[...]
    square[...] = pad_l
    square[0:NZC, 0:LEV] = lbuf[...]
    square[64 : 64 + NZC, 0:LEV] = lbuf[...]
    whole = square[...]
    high = whole.astype(BF16)
    rest = (whole - high.astype(F32)).astype(BF16)
    level2[:, 0:128] = high
    level2[:, 128:256] = high
    level2[:, 256:384] = rest
    square[...] = pad_l
    square[0:NZC, 0:LEV] = bbuf[...]
    square[64 : 64 + NZC, 0:LEV] = bbuf[...]
    whole = square[...]
    high = whole.astype(BF16)
    back2[0:128, :] = high
    back2[128:256, :] = (whole - high.astype(F32)).astype(BF16)
    row_c = iota((COLS, ROWS), 0)
    lane_r = iota((COLS, ROWS), 1)
    for f in range(FIELDS):
        value = jnp.zeros((COLS, ROWS), F32)
        for g in range(FIELDS):
            value = jnp.where(lane_r == row_c + g * COLS, coup[f, g], value)
        kron[f * COLS : (f + 1) * COLS, :] = value.astype(BF16)

    def forcing(window):
        hval = host[window]
        hval = jnp.where(lane < LEV, hval, 0.0)
        hhigh = hval.astype(BF16)
        hlow = (hval - hhigh.astype(F32)).astype(BF16)
        triple = jnp.concatenate([hhigh, hlow, hhigh], axis=1)
        mapped = lax.dot_general(triple, level2[...], NT, preferred_element_type=F32)
        high = mapped.astype(BF16).astype(F32)
        mhl = jnp.where(low, high, mapped - high)
        stack = jnp.concatenate([mhl] + [pltpu.roll(mhl, 128 - j, 1) for j in range(1, BLOCKS)], axis=0)
        cells = jnp.dot(stack.astype(BF16), spread_lanes, preferred_element_type=F32)
        for j in range(BLOCKS):
            for f in range(FIELDS):
                force[j, f * COLS : (f + 1) * COLS, :] = scale[f] * cells[j * COLS : (j + 1) * COLS, :]

    forcing(0)

    @pl.when(elem != 0)
    def _():
        send_borders()

    for f in range(FIELDS):
        loads[f].wait()
        rows = slice(f * COLS, (f + 1) * COLS)
        for j in range(BLOCKS):
            for half in range(2):
                za, zb = 30 * half + j, 30 * half + 15 + j
                ta = xbuf[f, :, (za // 2) * 128 : (za // 2 + 1) * 128]
                tb = xbuf[f, :, (zb // 2) * 128 : (zb // 2 + 1) * 128]
                if j % 2 == 0:
                    tile = jnp.where(low, ta, tb)
                else:
                    tile = swap_halves(jnp.where(low, tb, ta))
                sa[j, rows, half * 128 : (half + 1) * 128] = tile.astype(F32)

    def weighted(j):
        total = weight[0] * sa[j, 0:COLS, :]
        for f in range(1, FIELDS):
            total = total + weight[f] * sa[j, f * COLS : (f + 1) * COLS, :]
        return total

    for j in range(BLOCKS):
        qsum[j] = weighted(j)

    def shift_up(value):
        moved = pltpu.roll(value, NXC, 1)
        return jnp.where(lane_q < NXC, 0.0, moved)

    def shift_down(value):
        moved = pltpu.roll(value, LANES - NXC, 1)
        return jnp.where(lane_q >= LANES - NXC, 0.0, moved)

    cnt = jnp.broadcast_to(ccol, (COLS, LANES))

    def substep(src_ref, dst_ref, turn):
        a = jnp.where(cnt > turn.astype(F32), STEP, 0.0)
        keep = 1.0 - 2.0 * a

        for j0 in range(0, BLOCKS, 5):
            packed = jnp.concatenate([src_ref[j].astype(BF16) for j in range(j0, j0 + 5)], axis=0)
            slopes = jnp.dot(packed, deriv[...], preferred_element_type=F32)
            for j in range(j0, j0 + 5):
                mix = jnp.dot(kron[...], packed[(j - j0) * ROWS : (j - j0 + 1) * ROWS], preferred_element_type=F32)
                slope = slopes[(j - j0) * ROWS : (j - j0 + 1) * ROWS]
                wind = src_ref[j, 0:COLS]
                for f in range(FIELDS):
                    rows = slice(f * COLS, (f + 1) * COLS)
                    above = src_ref[j + 1, rows] if j < BLOCKS - 1 else shift_down(src_ref[0, rows])
                    below = src_ref[j - 1, rows] if j > 0 else shift_up(src_ref[BLOCKS - 1, rows])
                    total = (above + below) + (jnp.tanh(mix[rows]) + force[j, rows]) + wind * slope[rows]
                    dst_ref[j, rows] = keep * src_ref[j, rows] + a * total

    def fluxes(window, hval):
        def face(near):
            knear = jnp.broadcast_to(near[:, LEV : LEV + 1], (COLS, 128))
            return 0.5 * (kmid + knear) * (near - hval)

        prev = pltpu.roll(hval, 1, 0)
        prev = jnp.where(sub_row == 0, jnp.broadcast_to(halo_b[window, 0, 7:8, :], (COLS, 128)), prev)
        nxt = pltpu.roll(hval, COLS - 1, 0)
        nxt = jnp.where(sub_row == COLS - 1, jnp.broadcast_to(halo_b[window, 1, 0:1, :], (COLS, 128)), nxt)
        flux = face(halo_e[window, 1]) + face(halo_e[window, 0])
        return flux + face(nxt) + face(prev)

    def turns0(i, carry):
        substep(sa, sb, 2 * i)
        @pl.when(jnp.logical_and(elem == 0, i == 0))
        def _():
            send_borders()

        substep(sb, sa, 2 * i + 1)
        return carry

    lax.fori_loop(0, SUB // 2, turns0, 0)

    for j in range(BLOCKS):
        now = weighted(j)
        dq[j] = (now - qsum[j]).astype(BF16)
        qsum[j] = now
    for copy in exchange(0):
        copy.wait()
    hval = host[0]
    tend = tendency(dq, back2)
    hnew = hval + (tend + fluxes(0, hval))
    host[1] = jnp.where(lane == LEV, kmid, hnew)
    copies = exchange(1)
    for copy in copies:
        copy.start()
    forcing(1)

    def turns1(i, carry):
        substep(sa, sb, 2 * i)
        substep(sb, sa, 2 * i + 1)
        return carry

    lax.fori_loop(0, SUB // 2, turns1, 0)

    for j in range(BLOCKS):
        dq[j] = (weighted(j) - qsum[j]).astype(BF16)
    tend = tendency(dq, back2)
    for f in range(FIELDS):
        rows = slice(f * COLS, (f + 1) * COLS)
        tiles = {}
        for j in range(BLOCKS):
            for half in range(2):
                tile = sa[j, rows, half * 128 : (half + 1) * 128].astype(BF16)
                tiles[j, half] = tile if j % 2 == 0 else swap_halves(tile)
        for t in range(TILES):
            za, zb = 2 * t, 2 * t + 1
            ta = tiles[za % 15, za // 30]
            tb = tiles[zb % 15, zb // 30]
            obuf[f, :, t * 128 : (t + 1) * 128] = jnp.where(low, ta, tb)
    for copy in copies:
        copy.wait()
    hval = host[1]
    host_fin[...] = (hval + (tend + fluxes(1, hval)))[:, 0:LEV]


def tendency(dq, back2):
    rq = iota((LANES, 128), 0)
    cq = iota((LANES, 128), 1)
    gather_lanes = jnp.where(cq == 15 * (rq // NXC), 1.0 / NXC, 0.0).astype(BF16)
    parts = jnp.concatenate([dq[j] for j in range(BLOCKS)], axis=0)
    means = jnp.dot(parts, gather_lanes, preferred_element_type=F32)
    mixed = means[0:COLS]
    for j in range(1, BLOCKS):
        mixed = mixed + pltpu.roll(means[j * COLS : (j + 1) * COLS], j, 1)
    high = mixed.astype(BF16)
    both = high.astype(F32) + pltpu.roll(mixed - high.astype(F32), 64, 1)
    pair = jnp.concatenate([both.astype(BF16), high], axis=1)
    return jnp.dot(pair, back2[...], preferred_element_type=F32)


def finish(crm, host, crm_out, host_out, out_sem, host_sem):
    stores = [pltpu.make_async_copy(crm.at[f], crm_out.at[f], out_sem.at[f]) for f in range(FIELDS)]
    stores.append(pltpu.make_async_copy(host, host_out, host_sem))
    for copy in stores:
        copy.start()
    for copy in stores:
        copy.wait()


def body(
    crm_state, host_state, kappa, substeps, coupling, level_map, field_scale, back_map, back_weight
):
    crm = jnp.transpose(crm_state[0], (1, 0, 2))
    host = jnp.transpose(host_state[:, 0, :], (1, 0))
    back = jnp.transpose(back_map, (1, 0))
    vmem = pl.BlockSpec(memory_space=pltpu.VMEM)
    hbm = pl.BlockSpec(memory_space=pltpu.HBM)
    middle = pl.pallas_call(
        kernel,
        out_shape=(
            jax.ShapeDtypeStruct((FIELDS, COLS, CELLS), BF16),
            jax.ShapeDtypeStruct((COLS, LEV), F32),
        ),
        in_specs=[hbm] * 9,
        out_specs=(vmem,) * 2,
        scratch_shapes=[
            pltpu.VMEM((FIELDS, COLS, CELLS), BF16),
            pltpu.VMEM((BLOCKS, ROWS, LANES), F32),
            pltpu.VMEM((BLOCKS, ROWS, LANES), F32),
            pltpu.VMEM((BLOCKS, COLS, LANES), BF16),
            pltpu.VMEM((256, 128), BF16),
            pltpu.VMEM((BLOCKS, ROWS, LANES), F32),
            pltpu.VMEM((BLOCKS, COLS, LANES), F32),
            pltpu.VMEM((ROWS, ROWS), BF16),
            pltpu.VMEM((LANES, LANES), BF16),
            pltpu.VMEM((128, 3 * 128), BF16),
            pltpu.VMEM((128, 128), F32),
            pltpu.VMEM((WINDOWS, COLS, 128), F32),
            pltpu.VMEM((WINDOWS, 2, COLS, 128), F32),
            pltpu.VMEM((WINDOWS, 2, 8, 128), F32),
            pltpu.VMEM((COLS, LEV), F32),
            pltpu.VMEM((1, COLS), F32),
            pltpu.VMEM((1, COLS), jnp.int32),
            pltpu.VMEM((NZC, LEV), F32),
            pltpu.VMEM((NZC, LEV), F32),
            pltpu.SMEM((FIELDS, FIELDS), F32),
            pltpu.SMEM((FIELDS,), F32),
            pltpu.SMEM((FIELDS,), F32),
            pltpu.SemaphoreType.DMA((FIELDS,)),
            pltpu.SemaphoreType.DMA((8,)),
            pltpu.SemaphoreType.DMA((WINDOWS, 4)),
            pltpu.SemaphoreType.DMA((WINDOWS, 4)),
        ],
        compiler_params=pltpu.CompilerParams(
            collective_id=0, has_side_effects=True, vmem_limit_bytes=40 * 1024 * 1024
        ),
    )(*(
        pltpu.with_memory_space_constraint(x, pltpu.HBM)
        for x in (crm, host, kappa, substeps, level_map, back, coupling, field_scale, back_weight)
    ))
    crm_final, host_final = pl.pallas_call(
        finish,
        out_shape=(
            jax.ShapeDtypeStruct((FIELDS, COLS, CELLS), BF16),
            jax.ShapeDtypeStruct((COLS, LEV), F32),
        ),
        in_specs=[vmem] * 2,
        out_specs=(hbm, hbm),
        scratch_shapes=[
            pltpu.SemaphoreType.DMA((FIELDS,)),
            pltpu.SemaphoreType.DMA,
        ],
        compiler_params=pltpu.CompilerParams(vmem_limit_bytes=16 * 1024 * 1024),
    )(*middle)
    return (
        jnp.transpose(crm_final, (1, 0, 2))[None],
        jnp.transpose(host_final, (1, 0))[:, None, :],
    )


def solution(mesh):
    return jax.shard_map(
        body,
        mesh=mesh,
        in_specs=(
            P("elem", "band", None, None),
            P(None, "elem", "band"),
            P("elem", "band"),
            P("elem", "band"),
            P(),
            P(),
            P(),
            P(),
            P(),
        ),
        out_specs=(P("elem", "band", None, None), P(None, "elem", "band")),
        check_vma=False,
    )
```

```python
import jax
import jax.numpy as jnp
from jax import lax
from jax.experimental import pallas as pl
from jax.experimental.pallas import tpu as pltpu
from jax.sharding import PartitionSpec as P

LEV = 72
FIELDS = 6
NZC = 60
NXC = 64
SUB = 4
WINDOWS = 2
COLS = 32
ROWS = FIELDS * COLS
BLOCKS = 15
LANES = 256
TILES = 30
CELLS = NZC * NXC
STEP = 0.1
MESH = pl.DeviceIdType.MESH
F32 = jnp.float32
BF16 = jnp.bfloat16
NT = (((1,), (1,)), ((), ()))


def iota(shape, axis):
    return lax.broadcasted_iota(jnp.int32, shape, axis)


def to_column(row):
    eye = iota((COLS, COLS), 0) == iota((COLS, COLS), 1)
    return jnp.sum(jnp.where(eye, jnp.broadcast_to(row, (COLS, COLS)), 0.0), axis=1, keepdims=True)


def swap_halves(tile):
    return pltpu.roll(tile, 64, 1)


def kernel(
    crm_in, host_in, kappa_in, counts_in, level_in, back_in, coup_in, scale_in, weight_in,
    obuf, host_fin,
    xbuf, sa, sb, dq, back2, force, qsum, kron, deriv, level2, square, host, halo_e, halo_b,
    hbuf, kbuf, cbuf, lbuf, bbuf, coup, scale, weight,
    in_sem, arg_sem, send_sem, recv_sem,
):
    elem, band = lax.axis_index("elem"), lax.axis_index("band")
    n_elem, n_band = lax.axis_size("elem"), lax.axis_size("band")
    up_e = (lax.rem(elem + 1, n_elem), band)
    dn_e = (lax.rem(elem + n_elem - 1, n_elem), band)
    up_b = (elem, lax.rem(band + 1, n_band))
    dn_b = (elem, lax.rem(band + n_band - 1, n_band))

    small = [
        pltpu.make_async_copy(src, dst, arg_sem.at[i])
        for i, (src, dst) in enumerate((
            (host_in, hbuf), (level_in, lbuf), (scale_in, scale), (kappa_in, kbuf), (counts_in, cbuf),
            (weight_in, weight), (coup_in, coup), (back_in, bbuf),
        ))
    ]
    for copy in small:
        copy.start()
    loads = [pltpu.make_async_copy(crm_in.at[f], xbuf.at[f], in_sem.at[f]) for f in range(FIELDS)]
    for copy in loads:
        copy.start()

    barrier = pltpu.get_barrier_semaphore()
    for other in (up_e, dn_e, up_b, dn_b):
        pl.semaphore_signal(barrier, inc=1, device_id=other, device_id_type=MESH)

    def exchange(window):
        src = host.at[window]
        copies = []
        for i, (other, part, dst) in enumerate((
            (up_e, src, halo_e.at[window, 0]),
            (dn_e, src, halo_e.at[window, 1]),
            (up_b, src.at[pl.ds(COLS - 8, 8)], halo_b.at[window, 0]),
            (dn_b, src.at[pl.ds(0, 8)], halo_b.at[window, 1]),
        )):
            copies.append(pltpu.make_async_remote_copy(
                src_ref=part, dst_ref=dst,
                send_sem=send_sem.at[window, i], recv_sem=recv_sem.at[window, i],
                device_id=other, device_id_type=MESH,
            ))
        return copies

    def send_borders():
        pl.semaphore_wait(barrier, 4)
        for copy in exchange(0):
            copy.start()

    pad_l = jnp.zeros((128, 128), F32)
    src = iota((LANES, LANES), 0)
    dst = iota((LANES, LANES), 1)
    same = (src // NXC) == (dst // NXC)
    ahead = jnp.logical_and(same, (src % NXC) == (dst + 1) % NXC)
    behind = jnp.logical_and(same, (dst % NXC) == (src + 1) % NXC)
    deriv[...] = (jnp.where(behind, 0.5, 0.0) - jnp.where(ahead, 0.5, 0.0)).astype(BF16)
    zq = iota((128, LANES), 0)
    lq = iota((128, LANES), 1)
    spread_lanes = jnp.where((zq % 64) == 15 * (lq // NXC), 1.0, 0.0).astype(BF16)
    sub_row = iota((COLS, 128), 0)
    lane = iota((COLS, 128), 1)
    lane_q = iota((COLS, LANES), 1)
    low = lane < NXC

    for copy in small:
        copy.wait()

    kcol = to_column(kbuf[...])
    ccol = to_column(cbuf[...].astype(F32))
    kmid = jnp.broadcast_to(kcol, (COLS, 128))
    host[0] = jnp.where(lane == LEV, kmid, 0.0)
    host[0, :, 0:LEV] = hbuf[...]
    square[...] = pad_l
    square[0:NZC, 0:LEV] = lbuf[...]
    square[64 : 64 + NZC, 0:LEV] = lbuf[...]
    whole = square[...]
    high = whole.astype(BF16)
    rest = (whole - high.astype(F32)).astype(BF16)
    level2[:, 0:128] = high
    level2[:, 128:256] = high
    level2[:, 256:384] = rest
    square[...] = pad_l
    square[0:NZC, 0:LEV] = bbuf[...]
    square[64 : 64 + NZC, 0:LEV] = bbuf[...]
    whole = square[...]
    high = whole.astype(BF16)
    back2[0:128, :] = high
    back2[128:256, :] = (whole - high.astype(F32)).astype(BF16)
    row_c = iota((COLS, ROWS), 0)
    lane_r = iota((COLS, ROWS), 1)
    for f in range(FIELDS):
        value = jnp.zeros((COLS, ROWS), F32)
        for g in range(FIELDS):
            value = jnp.where(lane_r == row_c + g * COLS, coup[f, g], value)
        kron[f * COLS : (f + 1) * COLS, :] = value.astype(BF16)

    def forcing(window):
        hval = host[window]
        hval = jnp.where(lane < LEV, hval, 0.0)
        hhigh = hval.astype(BF16)
        hlow = (hval - hhigh.astype(F32)).astype(BF16)
        triple = jnp.concatenate([hhigh, hlow, hhigh], axis=1)
        mapped = lax.dot_general(triple, level2[...], NT, preferred_element_type=F32)
        high = mapped.astype(BF16).astype(F32)
        mhl = jnp.where(low, high, mapped - high)
        stack = jnp.concatenate([mhl] + [pltpu.roll(mhl, 128 - j, 1) for j in range(1, BLOCKS)], axis=0)
        cells = jnp.dot(stack.astype(BF16), spread_lanes, preferred_element_type=F32)
        for j in range(BLOCKS):
            for f in range(FIELDS):
                force[j, f * COLS : (f + 1) * COLS, :] = scale[f] * cells[j * COLS : (j + 1) * COLS, :]

    forcing(0)

    @pl.when(elem != 0)
    def _():
        send_borders()

    for f in range(FIELDS):
        loads[f].wait()
        rows = slice(f * COLS, (f + 1) * COLS)
        for j in range(BLOCKS):
            for half in range(2):
                za, zb = 30 * half + j, 30 * half + 15 + j
                ta = xbuf[f, :, (za // 2) * 128 : (za // 2 + 1) * 128]
                tb = xbuf[f, :, (zb // 2) * 128 : (zb // 2 + 1) * 128]
                if j % 2 == 0:
                    tile = jnp.where(low, ta, tb)
                else:
                    tile = swap_halves(jnp.where(low, tb, ta))
                sa[j, rows, half * 128 : (half + 1) * 128] = tile.astype(F32)

    def weighted(j):
        total = weight[0] * sa[j, 0:COLS, :]
        for f in range(1, FIELDS):
            total = total + weight[f] * sa[j, f * COLS : (f + 1) * COLS, :]
        return total

    for j in range(BLOCKS):
        qsum[j] = weighted(j)

    def shift_up(value):
        moved = pltpu.roll(value, NXC, 1)
        return jnp.where(lane_q < NXC, 0.0, moved)

    def shift_down(value):
        moved = pltpu.roll(value, LANES - NXC, 1)
        return jnp.where(lane_q >= LANES - NXC, 0.0, moved)

    cnt = jnp.broadcast_to(ccol, (COLS, LANES))

    def substep(src_ref, dst_ref, turn):
        a = jnp.where(cnt > turn.astype(F32), STEP, 0.0)
        keep = 1.0 - 2.0 * a

        for j0 in range(0, BLOCKS, 5):
            packed = jnp.concatenate([src_ref[j].astype(BF16) for j in range(j0, j0 + 5)], axis=0)
            slopes = jnp.dot(packed, deriv[...], preferred_element_type=F32)
            for j in range(j0, j0 + 5):
                mix = jnp.dot(kron[...], packed[(j - j0) * ROWS : (j - j0 + 1) * ROWS], preferred_element_type=F32)
                slope = slopes[(j - j0) * ROWS : (j - j0 + 1) * ROWS]
                wind = src_ref[j, 0:COLS]
                for f in range(FIELDS):
                    rows = slice(f * COLS, (f + 1) * COLS)
                    above = src_ref[j + 1, rows] if j < BLOCKS - 1 else shift_down(src_ref[0, rows])
                    below = src_ref[j - 1, rows] if j > 0 else shift_up(src_ref[BLOCKS - 1, rows])
                    total = (above + below) + (jnp.tanh(mix[rows]) + force[j, rows]) + wind * slope[rows]
                    dst_ref[j, rows] = keep * src_ref[j, rows] + a * total

    def fluxes(window, hval):
        def face(near):
            knear = jnp.broadcast_to(near[:, LEV : LEV + 1], (COLS, 128))
            return 0.5 * (kmid + knear) * (near - hval)

        prev = pltpu.roll(hval, 1, 0)
        prev = jnp.where(sub_row == 0, jnp.broadcast_to(halo_b[window, 0, 7:8, :], (COLS, 128)), prev)
        nxt = pltpu.roll(hval, COLS - 1, 0)
        nxt = jnp.where(sub_row == COLS - 1, jnp.broadcast_to(halo_b[window, 1, 0:1, :], (COLS, 128)), nxt)
        flux = face(halo_e[window, 1]) + face(halo_e[window, 0])
        return flux + face(nxt) + face(prev)

    def turns0(i, carry):
        substep(sa, sb, 2 * i)
        @pl.when(jnp.logical_and(elem == 0, i == 0))
        def _():
            send_borders()

        substep(sb, sa, 2 * i + 1)
        return carry

    lax.fori_loop(0, SUB // 2, turns0, 0)

    for j in range(BLOCKS):
        now = weighted(j)
        dq[j] = (now - qsum[j]).astype(BF16)
        qsum[j] = now
    tend = tendency(dq, back2)
    hval = host[0]
    first = exchange(0)
    for copy in first:
        copy.wait_recv()
    hnew = hval + (tend + fluxes(0, hval))
    host[1] = jnp.where(lane == LEV, kmid, hnew)
    copies = exchange(1)
    for copy in copies:
        copy.start()
    forcing(1)

    def turns1(i, carry):
        substep(sa, sb, 2 * i)
        substep(sb, sa, 2 * i + 1)
        return carry

    lax.fori_loop(0, SUB // 2, turns1, 0)

    for j in range(BLOCKS):
        dq[j] = (weighted(j) - qsum[j]).astype(BF16)
    tend = tendency(dq, back2)
    for f in range(FIELDS):
        rows = slice(f * COLS, (f + 1) * COLS)
        tiles = {}
        for j in range(BLOCKS):
            for half in range(2):
                tile = sa[j, rows, half * 128 : (half + 1) * 128].astype(BF16)
                tiles[j, half] = tile if j % 2 == 0 else swap_halves(tile)
        for t in range(TILES):
            za, zb = 2 * t, 2 * t + 1
            ta = tiles[za % 15, za // 30]
            tb = tiles[zb % 15, zb // 30]
            obuf[f, :, t * 128 : (t + 1) * 128] = jnp.where(low, ta, tb)
    for copy in first:
        copy.wait_send()
    for copy in copies:
        copy.wait()
    hval = host[1]
    host_fin[...] = (hval + (tend + fluxes(1, hval)))[:, 0:LEV]


def tendency(dq, back2):
    rq = iota((LANES, 128), 0)
    cq = iota((LANES, 128), 1)
    gather_lanes = jnp.where(cq == 15 * (rq // NXC), 1.0 / NXC, 0.0).astype(BF16)
    parts = jnp.concatenate([dq[j] for j in range(BLOCKS)], axis=0)
    means = jnp.dot(parts, gather_lanes, preferred_element_type=F32)
    mixed = means[0:COLS]
    for j in range(1, BLOCKS):
        mixed = mixed + pltpu.roll(means[j * COLS : (j + 1) * COLS], j, 1)
    high = mixed.astype(BF16)
    both = high.astype(F32) + pltpu.roll(mixed - high.astype(F32), 64, 1)
    pair = jnp.concatenate([both.astype(BF16), high], axis=1)
    return jnp.dot(pair, back2[...], preferred_element_type=F32)


def finish(crm, host, crm_out, host_out, out_sem, host_sem):
    stores = [pltpu.make_async_copy(crm.at[f], crm_out.at[f], out_sem.at[f]) for f in range(FIELDS)]
    stores.append(pltpu.make_async_copy(host, host_out, host_sem))
    for copy in stores:
        copy.start()
    for copy in stores:
        copy.wait()


def body(
    crm_state, host_state, kappa, substeps, coupling, level_map, field_scale, back_map, back_weight
):
    crm = jnp.transpose(crm_state[0], (1, 0, 2))
    host = jnp.transpose(host_state[:, 0, :], (1, 0))
    back = jnp.transpose(back_map, (1, 0))
    vmem = pl.BlockSpec(memory_space=pltpu.VMEM)
    hbm = pl.BlockSpec(memory_space=pltpu.HBM)
    middle = pl.pallas_call(
        kernel,
        out_shape=(
            jax.ShapeDtypeStruct((FIELDS, COLS, CELLS), BF16),
            jax.ShapeDtypeStruct((COLS, LEV), F32),
        ),
        in_specs=[hbm] * 9,
        out_specs=(vmem,) * 2,
        scratch_shapes=[
            pltpu.VMEM((FIELDS, COLS, CELLS), BF16),
            pltpu.VMEM((BLOCKS, ROWS, LANES), F32),
            pltpu.VMEM((BLOCKS, ROWS, LANES), F32),
            pltpu.VMEM((BLOCKS, COLS, LANES), BF16),
            pltpu.VMEM((256, 128), BF16),
            pltpu.VMEM((BLOCKS, ROWS, LANES), F32),
            pltpu.VMEM((BLOCKS, COLS, LANES), F32),
            pltpu.VMEM((ROWS, ROWS), BF16),
            pltpu.VMEM((LANES, LANES), BF16),
            pltpu.VMEM((128, 3 * 128), BF16),
            pltpu.VMEM((128, 128), F32),
            pltpu.VMEM((WINDOWS, COLS, 128), F32),
            pltpu.VMEM((WINDOWS, 2, COLS, 128), F32),
            pltpu.VMEM((WINDOWS, 2, 8, 128), F32),
            pltpu.VMEM((COLS, LEV), F32),
            pltpu.VMEM((1, COLS), F32),
            pltpu.VMEM((1, COLS), jnp.int32),
            pltpu.VMEM((NZC, LEV), F32),
            pltpu.VMEM((NZC, LEV), F32),
            pltpu.SMEM((FIELDS, FIELDS), F32),
            pltpu.SMEM((FIELDS,), F32),
            pltpu.SMEM((FIELDS,), F32),
            pltpu.SemaphoreType.DMA((FIELDS,)),
            pltpu.SemaphoreType.DMA((8,)),
            pltpu.SemaphoreType.DMA((WINDOWS, 4)),
            pltpu.SemaphoreType.DMA((WINDOWS, 4)),
        ],
        compiler_params=pltpu.CompilerParams(
            collective_id=0, has_side_effects=True, vmem_limit_bytes=40 * 1024 * 1024
        ),
    )(*(
        pltpu.with_memory_space_constraint(x, pltpu.HBM)
        for x in (crm, host, kappa, substeps, level_map, back, coupling, field_scale, back_weight)
    ))
    crm_final, host_final = pl.pallas_call(
        finish,
        out_shape=(
            jax.ShapeDtypeStruct((FIELDS, COLS, CELLS), BF16),
            jax.ShapeDtypeStruct((COLS, LEV), F32),
        ),
        in_specs=[vmem] * 2,
        out_specs=(hbm, hbm),
        scratch_shapes=[
            pltpu.SemaphoreType.DMA((FIELDS,)),
            pltpu.SemaphoreType.DMA,
        ],
        compiler_params=pltpu.CompilerParams(vmem_limit_bytes=16 * 1024 * 1024),
    )(*middle)
    return (
        jnp.transpose(crm_final, (1, 0, 2))[None],
        jnp.transpose(host_final, (1, 0))[:, None, :],
    )


def solution(mesh):
    return jax.shard_map(
        body,
        mesh=mesh,
        in_specs=(
            P("elem", "band", None, None),
            P(None, "elem", "band"),
            P("elem", "band"),
            P("elem", "band"),
            P(),
            P(),
            P(),
            P(),
            P(),
        ),
        out_specs=(P("elem", "band", None, None), P(None, "elem", "band")),
        check_vma=False,
    )
```
